32 devices in a mesh: seq: 8 (over y, x, core), head: 4 (over z).
Axes of the slice: x: 2, y: 2, z: 4, core: 2. Of those that a mesh axis runs over, the one named last changes fastest.
Arguments:
- q2: bfloat16 [2048, 4096], P('seq', 'head'), may hold values from -128 to 128
- k2: bfloat16 [2048, 512], P('seq', 'head'), may hold values from -6 to 6
- v2: bfloat16 [2048, 512], P('seq', 'head'), may hold values from -6 to 6
- hidden: bfloat16 [2048, 8192], P('seq', 'head'), may hold values from -120 to 120
- w_query: bfloat16 [8192, 4096], P(None, 'head'), may hold values from -0.0625 to 0.0625
- b_query: float32 [4096], P('head'), may hold values from -3 to 3
- w_key: bfloat16 [8192, 512], P(None, 'head'), may hold values from -0.0625 to 0.0625
- b_key: float32 [512], P('head'), may hold values from -3 to 3
- w_value: bfloat16 [8192, 512], P(None, 'head'), may hold values from -0.0625 to 0.0625
- b_value: float32 [512], P('head'), may hold values from -3 to 3
- kept_index: int32 [2048], P('seq'), may hold values from 0 to 127, as said below
- block_count: int32 [16], P('seq'), may hold values from 0 to 128, as said below
- text_rows: int32 [256], replicated, may hold values from 0 to 2047, as said below
Outputs:
- attn2: bfloat16 [2048, 4096], P('seq', 'head')
- importance: float32 [2048], P('seq')
- attn3: bfloat16 [1152, 4096], P('seq', 'head')
The draws below stay inside these ranges and needn't reach their ends.
Inputs may be any that keep to these rules, and one draw needn't show every extreme that they name: `kept_index`: in each aligned block of 128 rows, the first block_count entries are the in-block indices of that block's kept rows in ascending order; the other entries are the block's remaining indices. `block_count`: every text row is kept, and exactly 1152 rows are kept in all. For every k, the rows 2 * k * 256 to (2 * k + 2) * 256 - 1 hold exactly 288 kept rows together. `text_rows`: Distinct, in ascending order.
All inputs are finite; a program needn't handle non-finite values.
Results may differ from the reference program's by a relative error of at most 0.0093.
Values may be sent and summed in bfloat16 or wider, within the bound.
A program may use at most 128 MiB of HBM per device.

```python
import math
import jax
import jax.numpy as jnp
from jax import lax

D = 8192
HD = 128
GROUP = 8
KV_HEADS = 4
Q_HEADS = 32
ROWS_DEV = 256
BLOCK = 128
TEXT = 256
TOKENS = 2048
KEPT = 1152


def kept_layout(key):
    base = jax.random.fold_in(key, 7301)
    first, second, third = jax.random.split(base, 3)
    seq_count = TOKENS // ROWS_DEV
    share = TEXT // seq_count
    per_device = KEPT // seq_count
    starts = jax.random.randint(first, (seq_count,), 0, ROWS_DEV - share + 1)
    local = jnp.arange(ROWS_DEV, dtype=jnp.int32)[None, :]
    is_text = (local >= starts[:, None]) & (local < starts[:, None] + share)
    lower = jax.random.randint(second, (seq_count // 2,), share, ROWS_DEV + 1)
    counts_dev = jnp.stack([lower, 2 * per_device - lower], axis=1).reshape(-1)
    noise = jax.random.randint(third, (seq_count, ROWS_DEV), 0, 8192)
    priority = jnp.where(is_text, 3 * 8192, noise)
    distinct = priority * ROWS_DEV + local
    order_dev = jnp.argsort(-distinct, axis=1)
    rank = jnp.argsort(order_dev, axis=1)
    keep = (rank < counts_dev[:, None]).astype(jnp.int32).reshape(-1)
    grouped = keep.reshape(-1, BLOCK)
    counts = jnp.sum(grouped, axis=1).astype(jnp.int32)
    order = jnp.argsort(1 - grouped, axis=1, stable=True).astype(jnp.int32).reshape(-1)
    flat_text = is_text.reshape(-1).astype(jnp.int32)
    text_list = jnp.argsort(1 - flat_text, stable=True)[:TEXT].astype(jnp.int32)
    return (order, counts, text_list)


def draw_kept_index(key, part):
    return kept_layout(key)[0]


def draw_block_count(key, part):
    return kept_layout(key)[1]


def draw_text_rows(key, part):
    return kept_layout(key)[2]


def attention_inputs(key):
    base = jax.random.fold_in(key, 4211)
    first, second = jax.random.split(base, 2)
    queries = jax.random.truncated_normal(first, -6.0, 6.0, (TOKENS, Q_HEADS * HD), jnp.float32)
    keys = jax.random.truncated_normal(second, -6.0, 6.0, (TOKENS, KV_HEADS * HD), jnp.float32)
    return (queries, keys)


def draw_q2(key, part):
    return attention_inputs(key)[0].astype(jnp.bfloat16)


def draw_k2(key, part):
    return attention_inputs(key)[1].astype(jnp.bfloat16)


def draw_hidden(key, part):
    first = jax.random.fold_in(jax.random.fold_in(key, 5519), 0)
    states = jax.random.truncated_normal(first, -6.0, 6.0, (TOKENS, D), jnp.float32)
    return states.astype(jnp.bfloat16)


def block_scale(rng, dims, shards, least, top_value):
    gain = 1.0
    for dim, blocks in shards:
        heights = jax.random.uniform(jax.random.fold_in(jax.random.fold_in(rng, 6), dim), (blocks,), jnp.float32, least / len(shards), top_value / len(shards))
        gain = gain * jnp.repeat(jnp.exp(heights), dims[dim] // blocks).reshape((-1,) + (1,) * (len(dims) - 1 - dim))
    return gain


def centred(stream_key, shape, scale, limit, cuts=(), held_as=jnp.bfloat16):
    result = scale * jax.random.normal(stream_key, shape, jnp.float32)
    if cuts:
        result = result * block_scale(stream_key, shape, cuts, -0.22, 0.18)
    return jnp.clip(result, -limit, limit).astype(held_as)


def setup_inputs(seed: int = 0) -> dict:
    arg_keys = jax.random.split(jax.random.key(seed), 14)
    return {
        "q2": draw_q2(jax.random.fold_in(arg_keys[13], 71), 0),
        "k2": draw_k2(jax.random.fold_in(arg_keys[13], 71), 0),
        "v2": centred(arg_keys[2], (TOKENS, KV_HEADS * HD), 1.0, 6.0, ((0, 8), (1, 4))),
        "hidden": draw_hidden(jax.random.fold_in(arg_keys[13], 71), 0),
        "w_query": centred(arg_keys[4], (D, Q_HEADS * HD), D ** -0.5, 0.0625, ((1, 4),)),
        "b_query": centred(arg_keys[5], (Q_HEADS * HD,), 0.5, 3.0, ((0, 4),), jnp.float32),
        "w_key": centred(arg_keys[6], (D, KV_HEADS * HD), D ** -0.5, 0.0625, ((1, 4),)),
        "b_key": centred(arg_keys[7], (KV_HEADS * HD,), 0.5, 3.0, ((0, 4),), jnp.float32),
        "w_value": centred(arg_keys[8], (D, KV_HEADS * HD), D ** -0.5, 0.0625, ((1, 4),)),
        "b_value": centred(arg_keys[9], (KV_HEADS * HD,), 0.5, 3.0, ((0, 4),), jnp.float32),
        "kept_index": draw_kept_index(jax.random.fold_in(arg_keys[13], 71), 0),
        "block_count": draw_block_count(jax.random.fold_in(arg_keys[13], 71), 0),
        "text_rows": draw_text_rows(jax.random.fold_in(arg_keys[13], 71), 0),
    }


def rotate(values, positions):
    half = values.shape[-1] // 2
    freqs = 1000000.0 ** (-(jnp.arange(half, dtype=jnp.float32) * 2.0) / values.shape[-1])
    angles = positions.astype(jnp.float32)[:, None] * freqs[None, :]
    cosine = jnp.cos(angles)[:, None, :]
    sine = jnp.sin(angles)[:, None, :]
    first = values[..., :half]
    second = values[..., half:]
    return jnp.concatenate([first * cosine - second * sine, second * cosine + first * sine], axis=-1)

def causal_block(queries, keys, values, query_pos, key_pos):
    scores = jnp.einsum('qagd,kad->agqk', queries, keys) / math.sqrt(HD)
    allowed = key_pos[None, :] <= query_pos[:, None]
    top = lax.optimization_barrier(jnp.max(jnp.where(allowed, scores, -1e+30), axis=-1))
    weights = jnp.where(allowed, jnp.exp(scores - top[..., None]), 0.0)
    total = lax.optimization_barrier(jnp.sum(weights, axis=-1))
    rounded = weights.astype(jnp.bfloat16).astype(jnp.float32)
    summed = jnp.einsum('agqk,kad->qagd', rounded, values)
    return (summed / jnp.transpose(total, (2, 0, 1))[..., None], top, total)

def attention(queries, keys, values, positions):
    count = queries.shape[0]
    width = math.gcd(count, 256)

    def one_block(start):
        block = lax.dynamic_slice_in_dim(queries, start, width, 0)
        query_pos = lax.dynamic_slice_in_dim(positions, start, width, 0)
        out, top, total = causal_block(block, keys, values, query_pos, positions)
        return out.reshape(width, -1).astype(jnp.bfloat16)
    starts = jnp.arange(0, count, width, dtype=jnp.int32)
    return lax.map(one_block, starts).reshape(count, -1)

def reference(q2, k2, v2, hidden, w_query, b_query, w_key, b_key, w_value, b_value, kept_index, block_count, text_rows):
    positions = jnp.arange(TOKENS, dtype=jnp.int32)
    queries = q2.astype(jnp.float32).reshape(TOKENS, KV_HEADS, GROUP, HD)
    keys = k2.astype(jnp.float32).reshape(TOKENS, KV_HEADS, HD)
    values = v2.astype(jnp.float32).reshape(TOKENS, KV_HEADS, HD)
    attn2 = attention(queries, keys, values, positions)
    text_queries = queries[text_rows]
    _, top, total = causal_block(text_queries, keys, values, text_rows, positions)
    scores = jnp.einsum('tagd,kad->agtk', text_queries, keys) / math.sqrt(HD)
    allowed = positions[None, :] <= text_rows[:, None]
    probs = jnp.where(allowed, jnp.exp(scores - top[..., None]) / total[..., None], 0.0)
    importance = lax.optimization_barrier(jnp.sum(probs, axis=(0, 1, 2))) * (TOKENS / (Q_HEADS * TEXT))
    index_list = kept_index.reshape(-1, BLOCK)
    live = jnp.arange(BLOCK, dtype=jnp.int32)[None, :] < block_count[:, None]
    marks = jnp.any(live[:, :, None] & (index_list[:, :, None] == jnp.arange(BLOCK, dtype=jnp.int32)[None, None, :]), axis=1)
    flags = marks.reshape(TOKENS).astype(jnp.int32)
    kept_pos = jnp.argsort(1 - flags, stable=True)[:KEPT].astype(jnp.int32)
    rows = hidden[kept_pos]
    query_three = jnp.dot(rows, w_query, preferred_element_type=jnp.float32) + b_query
    query_three = rotate(query_three.reshape(KEPT, Q_HEADS, HD), kept_pos).astype(jnp.bfloat16)
    key_three = jnp.dot(rows, w_key, preferred_element_type=jnp.float32) + b_key
    key_three = rotate(key_three.reshape(KEPT, KV_HEADS, HD), kept_pos).astype(jnp.bfloat16)
    value_three = (jnp.dot(rows, w_value, preferred_element_type=jnp.float32) + b_value).astype(jnp.bfloat16)
    order = jnp.arange(KEPT, dtype=jnp.int32)
    attn3 = attention(query_three.astype(jnp.float32).reshape(KEPT, KV_HEADS, GROUP, HD), key_three.astype(jnp.float32).reshape(KEPT, KV_HEADS, HD), value_three.astype(jnp.float32).reshape(KEPT, KV_HEADS, HD), order)
    return (attn2, importance, attn3)
```

```python
import functools
import math

import jax
import jax.numpy as jnp
from jax import lax
from jax.experimental import pallas as pl
from jax.experimental.pallas import tpu as pltpu
from jax.sharding import PartitionSpec as P

HD = 128
GROUP = 8
BLOCK = 128
THETA = 1000000.0


def chunk_width(count):
    width = 512
    while count % width:
        width -= 128
    return width


def loop(count, step, carry):
    if count <= 4:
        for turn in range(count):
            carry = step(turn, carry)
        return carry
    return lax.fori_loop(0, count, step, carry)


def attention_kernel(weigh, start_ref, q_ref, k_ref, v_ref, *rest):
    if weigh:
        text_ref, out_ref, imp_ref, score = rest
    else:
        out_ref, score = rest
    rows = q_ref.shape[0]
    count = k_ref.shape[0]
    width = score.shape[2]
    chunks = count // width
    queries = q_ref[...]
    row = start_ref[0] + lax.broadcasted_iota(jnp.int32, (rows, width), 0)
    ahead = row - lax.broadcasted_iota(jnp.int32, (rows, width), 1)
    scale = 1.0 / math.sqrt(HD)

    def span(turn):
        return pl.ds(pl.multiple_of(turn * width, 128), width)

    def first(turn, top):
        scores = lax.dot_general(
            queries, k_ref[span(turn), :], (((1,), (1,)), ((), ())), preferred_element_type=jnp.float32
        )
        scores = jnp.where(ahead >= turn * width, scores, -1e30)
        score[turn] = scores
        for part in range(width // 128):
            top = jnp.maximum(top, scores[:, part * 128 : (part + 1) * 128])
        return top

    top = loop(chunks, first, jnp.full((rows, 128), -1e30, jnp.float32))
    top = jnp.max(top, axis=1, keepdims=True)

    def second(turn, state):
        total, summed = state
        weights = jnp.exp((score[turn] - top) * scale)
        if weigh:
            score[turn] = weights
        for part in range(width // 128):
            total = total + weights[:, part * 128 : (part + 1) * 128]
        summed = summed + jnp.dot(
            weights.astype(jnp.bfloat16), v_ref[span(turn), :], preferred_element_type=jnp.float32
        )
        return (total, summed)

    blank = jnp.zeros((rows, 128), jnp.float32)
    total, summed = loop(chunks, second, (blank, blank))
    inverse = 1.0 / jnp.sum(total, axis=1, keepdims=True)
    out_ref[...] = (summed * inverse).astype(jnp.bfloat16)
    if weigh:

        @pl.when(pl.program_id(0) == 0)
        def _():
            imp_ref[...] = jnp.zeros_like(imp_ref)

        share = inverse * text_ref[...]

        def third(turn, state):
            part = jnp.sum(score[turn] * share, axis=0, keepdims=True)
            imp_ref[:, span(turn)] += part
            return state

        loop(chunks, third, 0)


def attention(start, queries, keys, values, text=None):
    rows, columns = queries.shape
    heads = columns // HD
    count = keys.shape[0]
    width = chunk_width(count)
    weigh = text is not None
    head_spec = pl.BlockSpec((rows, HD), lambda h, s: (0, h))
    whole = lambda shape: pl.BlockSpec(shape, lambda h, s: (0, 0))
    in_specs = [head_spec, whole((count, HD)), whole((count, HD))]
    operands = [queries, keys, values]
    out_shape = [jax.ShapeDtypeStruct((rows, columns), jnp.bfloat16)]
    out_specs = [head_spec]
    if weigh:
        in_specs.append(whole((rows, 1)))
        operands.append(text)
        out_shape.append(jax.ShapeDtypeStruct((1, count), jnp.float32))
        out_specs.append(whole((1, count)))
    return pl.pallas_call(
        functools.partial(attention_kernel, weigh),
        grid_spec=pltpu.PrefetchScalarGridSpec(
            num_scalar_prefetch=1,
            grid=(heads,),
            in_specs=in_specs,
            out_specs=out_specs,
            scratch_shapes=[pltpu.VMEM((count // width, rows, width), jnp.float32)],
        ),
        out_shape=out_shape,
        compiler_params=pltpu.CompilerParams(vmem_limit_bytes=40 * 1024 * 1024),
        cost_estimate=pl.CostEstimate(
            flops=4 * rows * columns * count, bytes_accessed=4 * rows * columns, transcendentals=rows * heads * count
        ),
    )(start.reshape(1), *operands)


def project_kernel(
    x_ref, wq_ref, wk_ref, wv_ref, bias_ref, cos_ref, sin_ref, q_ref, kv_ref, acc_q, acc_k, acc_v
):
    @pl.when(pl.program_id(0) == 0)
    def _():
        columns = acc_q.shape[1]
        acc_q[...] = jnp.broadcast_to(bias_ref[:, :columns], acc_q.shape)
        acc_k[...] = jnp.broadcast_to(bias_ref[:, columns : columns + HD], acc_k.shape)
        acc_v[...] = jnp.broadcast_to(bias_ref[:, columns + HD :], acc_v.shape)

    x = x_ref[...]
    acc_q[...] += jnp.dot(x, wq_ref[...], preferred_element_type=jnp.float32)
    acc_k[...] += jnp.dot(x, wk_ref[...], preferred_element_type=jnp.float32)
    acc_v[...] += jnp.dot(x, wv_ref[...], preferred_element_type=jnp.float32)

    @pl.when(pl.program_id(0) == pl.num_programs(0) - 1)
    def _():
        cosine, sine = cos_ref[...], sin_ref[...]

        def turned(u):
            return (u * cosine + pltpu.roll(u, HD // 2, 1) * sine).astype(jnp.bfloat16)

        for head in range(acc_q.shape[1] // HD):
            part = slice(head * HD, (head + 1) * HD)
            q_ref[:, part] = turned(acc_q[:, part])
        kv_ref[:, :HD] = turned(acc_k[...])
        kv_ref[:, HD:] = acc_v[...].astype(jnp.bfloat16)


def project(x, cosine, sine, w_query, w_key, w_value, bias):
    rows, depth = x.shape
    columns = w_query.shape[1]
    step = 1024
    whole = lambda shape: pl.BlockSpec(shape, lambda i: (0, 0))
    down = lambda width: pl.BlockSpec((step, width), lambda i: (i, 0))
    return pl.pallas_call(
        project_kernel,
        grid=(depth // step,),
        in_specs=[
            pl.BlockSpec((rows, step), lambda i: (0, i)),
            down(columns),
            down(HD),
            down(HD),
            whole((1, columns + 2 * HD)),
            whole((rows, HD)),
            whole((rows, HD)),
        ],
        out_specs=[whole((rows, columns)), whole((rows, 2 * HD))],
        out_shape=[
            jax.ShapeDtypeStruct((rows, columns), jnp.bfloat16),
            jax.ShapeDtypeStruct((rows, 2 * HD), jnp.bfloat16),
        ],
        scratch_shapes=[
            pltpu.VMEM((rows, columns), jnp.float32),
            pltpu.VMEM((rows, HD), jnp.float32),
            pltpu.VMEM((rows, HD), jnp.float32),
        ],
        compiler_params=pltpu.CompilerParams(vmem_limit_bytes=32 * 1024 * 1024),
        cost_estimate=pl.CostEstimate(
            flops=2 * rows * depth * (columns + 2 * HD),
            bytes_accessed=2 * depth * (columns + 2 * HD),
            transcendentals=0,
        ),
    )(x, w_query, w_key, w_value, bias, cosine, sine)


def body(
    q2, k2, v2, hidden, w_query, b_query, w_key, b_key, w_value, b_value, kept_index, block_count, text_rows
):
    rows = q2.shape[0]
    seq_count = lax.axis_size("seq")
    head_count = lax.axis_size("head")
    seq_rank = lax.axis_index("seq")
    first_row = seq_rank * rows
    text = text_rows.shape[0]
    per_device = (rows * seq_count + text) // (2 * seq_count)
    odd = seq_rank % 2

    blocks = rows // BLOCK
    ends = [block_count[0]]
    for b in range(1, blocks):
        ends.append(ends[-1] + block_count[b])
    kept_count = ends[-1]
    base = jnp.where(odd == 1, 2 * per_device - kept_count, 0)
    entry = jnp.arange(rows, dtype=jnp.int32)
    place = base + entry % BLOCK
    live = jnp.zeros((rows,), jnp.bool_)
    for b in range(blocks):
        inside = entry // BLOCK == b
        begin = ends[b] - block_count[b]
        place = place + jnp.where(inside, begin, 0)
        live = live | (inside & (entry % BLOCK < block_count[b]))
    source = (entry // BLOCK) * BLOCK + kept_index

    def window(start, count):
        order = start + jnp.arange(count, dtype=jnp.int32)
        hit = (order[:, None] == place[None, :]) & live[None, :]
        chosen = jnp.sum(jnp.where(hit, source[None, :] + 1, 0), axis=1) - 1
        select = (chosen[:, None] == jnp.arange(rows, dtype=jnp.int32)[None, :]).astype(jnp.bfloat16)
        picked = jnp.dot(select, hidden, preferred_element_type=jnp.float32).astype(jnp.bfloat16)
        return picked, jnp.where(chosen >= 0, chosen + first_row, 0)

    span = min(rows - per_device, per_device)
    swap = [(i, i + 1 - 2 * (i % 2)) for i in range(seq_count)]
    sent_rows, sent_pos = window(jnp.where(odd == 1, per_device - span, per_device), span)
    got_rows = lax.ppermute(sent_rows, "seq", swap)
    got_pos = lax.ppermute(sent_pos, "seq", swap)
    own_rows, own_pos = window(odd * per_device, per_device)
    rest = per_device - span
    low = jnp.where(odd == 1, 0, rest)

    def landed(got):
        shape = ((0, rest),) + ((0, 0),) * (got.ndim - 1)
        back = ((rest, 0),) + ((0, 0),) * (got.ndim - 1)
        return jnp.where(odd == 1, jnp.pad(got, shape), jnp.pad(got, back))

    kept_rows = own_rows + landed(got_rows)
    kept_pos = own_pos + landed(got_pos)
    full_rows = lax.all_gather(kept_rows, "head", axis=1, tiled=True)

    pairs = lax.all_gather(jnp.concatenate([k2, v2], axis=1), "seq", axis=0, tiled=True)
    query_pos = first_row + jnp.arange(rows, dtype=jnp.int32)
    is_text = jnp.any(query_pos[:, None] == text_rows[None, :], axis=1, keepdims=True).astype(jnp.float32)
    attn2, partial_value = attention(first_row, q2, pairs[:, :HD], pairs[:, HD:], is_text)
    head_total = lax.psum(partial_value.reshape(-1), ("seq", "head"))
    importance = lax.dynamic_slice_in_dim(head_total, first_row, rows, 0) * (
        rows * seq_count / (GROUP * head_count * text)
    )

    half = HD // 2
    freqs = THETA ** (-(jnp.arange(half, dtype=jnp.float32) * 2.0) / HD)
    angles = kept_pos.astype(jnp.float32)[:, None] * freqs[None, :]
    cosine, sine = jnp.cos(angles), jnp.sin(angles)
    cosine = jnp.concatenate([cosine, cosine], axis=1)
    sine = jnp.concatenate([-sine, sine], axis=1)
    bias = jnp.concatenate([b_query, b_key, b_value])[None, :]
    queries3, pair3 = project(full_rows, cosine, sine, w_query, w_key, w_value, bias)
    pairs3 = lax.all_gather(pair3, "seq", axis=0, tiled=True)
    (attn3,) = attention(seq_rank * per_device, queries3, pairs3[:, :HD], pairs3[:, HD:])
    return (attn2, importance, attn3)


def solution(mesh):
    placed = (
        P("seq", "head"),
        P("seq", "head"),
        P("seq", "head"),
        P("seq", "head"),
        P(None, "head"),
        P("head"),
        P(None, "head"),
        P("head"),
        P(None, "head"),
        P("head"),
        P("seq"),
        P("seq"),
        P(),
    )
    return jax.shard_map(
        body,
        mesh=mesh,
        in_specs=placed,
        out_specs=(P("seq", "head"), P("seq"), P("seq", "head")),
        check_vma=False,
    )
```

```python
import functools
import math

import jax
import jax.numpy as jnp
from jax import lax
from jax.experimental import pallas as pl
from jax.experimental.pallas import tpu as pltpu
from jax.sharding import PartitionSpec as P

HD = 128
GROUP = 8
BLOCK = 128
THETA = 1000000.0


def chunk_width(count):
    width = 512
    while count % width:
        width -= 128
    return width


def loop(count, step, carry):
    if count <= 8:
        for turn in range(count):
            carry = step(turn, carry)
        return carry
    return lax.fori_loop(0, count, step, carry)


def attention_kernel(weigh, start_ref, q_ref, k_ref, v_ref, *rest):
    if weigh:
        text_ref, out_ref, imp_ref, score = rest
    else:
        out_ref, score = rest
    rows = q_ref.shape[0]
    count = k_ref.shape[0]
    width = score.shape[2]
    chunks = count // width
    queries = q_ref[...]
    row = start_ref[0] + lax.broadcasted_iota(jnp.int32, (rows, width), 0)
    ahead = row - lax.broadcasted_iota(jnp.int32, (rows, width), 1)
    scale = 1.0 / math.sqrt(HD)

    def span(turn):
        return pl.ds(pl.multiple_of(turn * width, 128), width)

    def first(turn, top):
        scores = lax.dot_general(
            queries, k_ref[span(turn), :], (((1,), (1,)), ((), ())), preferred_element_type=jnp.float32
        )
        scores = jnp.where(ahead >= turn * width, scores, -1e30)
        score[turn] = scores
        for part in range(width // 128):
            top = jnp.maximum(top, scores[:, part * 128 : (part + 1) * 128])
        return top

    top = loop(chunks, first, jnp.full((rows, 128), -1e30, jnp.float32))
    top = jnp.max(top, axis=1, keepdims=True)

    def second(turn, state):
        total, summed = state
        weights = jnp.exp((score[turn] - top) * scale)
        if weigh:
            score[turn] = weights
        for part in range(width // 128):
            total = total + weights[:, part * 128 : (part + 1) * 128]
        summed = summed + jnp.dot(
            weights.astype(jnp.bfloat16), v_ref[span(turn), :], preferred_element_type=jnp.float32
        )
        return (total, summed)

    blank = jnp.zeros((rows, 128), jnp.float32)
    total, summed = loop(chunks, second, (blank, blank))
    inverse = 1.0 / jnp.sum(total, axis=1, keepdims=True)
    out_ref[...] = (summed * inverse).astype(jnp.bfloat16)
    if weigh:

        @pl.when(pl.program_id(0) == 0)
        def _():
            imp_ref[...] = jnp.zeros_like(imp_ref)

        share = inverse * text_ref[...]

        def third(turn, state):
            part = jnp.sum(score[turn] * share, axis=0, keepdims=True)
            imp_ref[:, span(turn)] += part
            return state

        loop(chunks, third, 0)


def attention(start, queries, keys, values, text=None):
    rows, columns = queries.shape
    heads = columns // HD
    count = keys.shape[0]
    width = chunk_width(count)
    weigh = text is not None
    head_spec = pl.BlockSpec((rows, HD), lambda h, s: (0, h))
    whole = lambda shape: pl.BlockSpec(shape, lambda h, s: (0, 0))
    in_specs = [head_spec, whole((count, HD)), whole((count, HD))]
    operands = [queries, keys, values]
    out_shape = [jax.ShapeDtypeStruct((rows, columns), jnp.bfloat16)]
    out_specs = [head_spec]
    if weigh:
        in_specs.append(whole((rows, 1)))
        operands.append(text)
        out_shape.append(jax.ShapeDtypeStruct((1, count), jnp.float32))
        out_specs.append(whole((1, count)))
    return pl.pallas_call(
        functools.partial(attention_kernel, weigh),
        grid_spec=pltpu.PrefetchScalarGridSpec(
            num_scalar_prefetch=1,
            grid=(heads,),
            in_specs=in_specs,
            out_specs=out_specs,
            scratch_shapes=[pltpu.VMEM((count // width, rows, width), jnp.float32)],
        ),
        out_shape=out_shape,
        compiler_params=pltpu.CompilerParams(vmem_limit_bytes=40 * 1024 * 1024),
        cost_estimate=pl.CostEstimate(
            flops=4 * rows * columns * count, bytes_accessed=4 * rows * columns, transcendentals=rows * heads * count
        ),
    )(start.reshape(1), *operands)


MESH = pl.DeviceIdType.MESH


def fused_kernel(
    seq_count, head_count,
    q_ref, kv_ref, text_ref, x_ref, bias_ref, cos_ref, sin_ref, wq_ref, wk_ref, wv_ref,
    attn_ref, imp_ref, q3_ref, kv3_ref,
    kv_all, x_all, score, parts, part_all, mine, mine_all, wq, wk, wv, acc_q, acc_k, acc_v,
    kv_send, kv_recv, x_send, x_recv, p_send, p_recv, m_send, m_recv, w_sem,
):
    seq, head = lax.axis_index("seq"), lax.axis_index("head")
    rows = q_ref.shape[0]
    depth = x_ref.shape[1]
    columns = q_ref.shape[1]
    scale = 1.0 / math.sqrt(HD)

    def weights_in(turn):
        owner = lax.rem(head + turn, head_count)
        span = pl.ds(pl.multiple_of(owner * depth, 128), depth)
        pairs = ((wq_ref, wq), (wk_ref, wk), (wv_ref, wv))
        return [pltpu.make_async_copy(f.at[span, :], t.at[turn], w_sem.at[turn, i]) for i, (f, t) in enumerate(pairs)]

    for turn in range(head_count):
        for copy in weights_in(turn):
            copy.start()

    def seq_peer(k):
        return lax.rem(seq + k, seq_count)

    def head_peer(k):
        return lax.rem(head + k, head_count)

    barrier = pltpu.get_barrier_semaphore()
    for k in range(1, seq_count):
        pl.semaphore_signal(barrier, inc=1, device_id=(seq_peer(k), head), device_id_type=MESH)
    for k in range(1, head_count):
        pl.semaphore_signal(barrier, inc=1, device_id=(seq, head_peer(k)), device_id_type=MESH)
    pl.semaphore_wait(barrier, seq_count + head_count - 2)

    def kv_copy(k):
        return pltpu.make_async_remote_copy(
            src_ref=kv_ref, dst_ref=kv_all.at[seq_count - k], send_sem=kv_send.at[k],
            recv_sem=kv_recv.at[seq_count - k], device_id=(seq_peer(k), head), device_id_type=MESH,
        )

    def x_copy(k):
        return pltpu.make_async_remote_copy(
            src_ref=x_ref, dst_ref=x_all.at[head_count - k], send_sem=x_send.at[k],
            recv_sem=x_recv.at[head_count - k], device_id=(seq, head_peer(k)), device_id_type=MESH,
        )

    def part_copy(k):
        return pltpu.make_async_remote_copy(
            src_ref=parts.at[k], dst_ref=part_all.at[seq_count - k], send_sem=p_send.at[k],
            recv_sem=p_recv.at[seq_count - k], device_id=(seq_peer(k), head), device_id_type=MESH,
        )

    def mine_copy(k):
        return pltpu.make_async_remote_copy(
            src_ref=mine, dst_ref=mine_all.at[head_count - k], send_sem=m_send.at[k],
            recv_sem=m_recv.at[head_count - k], device_id=(seq, head_peer(k)), device_id_type=MESH,
        )

    for k in range(1, seq_count):
        kv_copy(k).start()
    for k in range(1, head_count):
        x_copy(k).start()
    kv_all[0] = kv_ref[...]
    parts[...] = jnp.zeros_like(parts)

    for copy in weights_in(0):
        copy.wait()
    x = x_ref[...]
    acc_q[...] = bias_ref[:, :columns] + jnp.dot(x, wq[0], preferred_element_type=jnp.float32)
    acc_k[...] = bias_ref[:, columns : columns + HD] + jnp.dot(x, wk[0], preferred_element_type=jnp.float32)
    acc_v[...] = bias_ref[:, columns + HD :] + jnp.dot(x, wv[0], preferred_element_type=jnp.float32)
    for k in range(1, seq_count):
        kv_copy(k).wait_recv()

    row = seq * rows + lax.broadcasted_iota(jnp.int32, (rows, rows), 0)
    ahead = row - lax.broadcasted_iota(jnp.int32, (rows, rows), 1)

    def one_head(h, state):
        span = pl.ds(pl.multiple_of(h * HD, 128), HD)
        queries = q_ref[:, span]

        def first(k, top):
            scores = lax.dot_general(
                queries, kv_all[k, :, :HD], (((1,), (1,)), ((), ())), preferred_element_type=jnp.float32
            )
            scores = jnp.where(ahead >= seq_peer(k) * rows, scores, -1e30)
            score[k] = scores
            for part in range(rows // 128):
                top = jnp.maximum(top, scores[:, part * 128 : (part + 1) * 128])
            return top

        top = loop(seq_count, first, jnp.full((rows, 128), -1e30, jnp.float32))
        top = jnp.max(top, axis=1, keepdims=True)

        def second(k, carry):
            total, summed = carry
            weights = jnp.exp((score[k] - top) * scale)
            score[k] = weights
            for part in range(rows // 128):
                total = total + weights[:, part * 128 : (part + 1) * 128]
            summed = summed + jnp.dot(
                weights.astype(jnp.bfloat16), kv_all[k, :, HD:], preferred_element_type=jnp.float32
            )
            return (total, summed)

        blank = jnp.zeros((rows, 128), jnp.float32)
        total, summed = loop(seq_count, second, (blank, blank))
        inverse = 1.0 / jnp.sum(total, axis=1, keepdims=True)
        attn_ref[:, span] = (summed * inverse).astype(jnp.bfloat16)
        share = inverse * text_ref[...]

        def third(k, carry):
            parts[k] += jnp.sum((score[k] * share).reshape(rows // 8, 8, rows), axis=0)
            return carry

        loop(seq_count, third, 0)
        return state

    lax.fori_loop(0, columns // HD, one_head, 0)
    for turn in range(1, head_count):
        for copy in weights_in(turn):
            copy.wait()
        x_copy(head_count - turn).wait_recv()
        x = x_all[turn]
        acc_q[...] += jnp.dot(x, wq[turn], preferred_element_type=jnp.float32)
        acc_k[...] += jnp.dot(x, wk[turn], preferred_element_type=jnp.float32)
        acc_v[...] += jnp.dot(x, wv[turn], preferred_element_type=jnp.float32)
        if turn == 1:
            for k in range(1, seq_count):
                part_copy(k).start()
        if turn == head_count - 1:
            gathered = parts[0]
            for k in range(1, seq_count):
                part_copy(k).wait_recv()
            for k in range(1, seq_count):
                gathered = gathered + part_all[k]
            mine[...] = gathered

    cosine, sine = cos_ref[...], sin_ref[...]

    def turned(u):
        return (u * cosine + pltpu.roll(u, HD // 2, 1) * sine).astype(jnp.bfloat16)

    for h in range(columns // HD):
        part = slice(h * HD, (h + 1) * HD)
        q3_ref[:, part] = turned(acc_q[:, part])
    kv3_ref[:, :HD] = turned(acc_k[...])
    kv3_ref[:, HD:] = acc_v[...].astype(jnp.bfloat16)
    for k in range(1, head_count):
        mine_copy(k).start()
    everyone = mine[...]
    for k in range(1, head_count):
        mine_copy(k).wait_recv()
    for k in range(1, head_count):
        everyone = everyone + mine_all[k]
    imp_ref[...] = everyone
    for k in range(1, seq_count):
        kv_copy(k).wait_send()
        part_copy(k).wait_send()
    for k in range(1, head_count):
        x_copy(k).wait_send()
        mine_copy(k).wait_send()


def fused(seq_count, head_count, q2, kv2, text, x, bias, cosine, sine, w_query, w_key, w_value):
    rows, columns = q2.shape
    kept, depth = x.shape
    vmem = pl.BlockSpec(memory_space=pltpu.VMEM)
    hbm = pl.BlockSpec(memory_space=pl.ANY)
    dma = pltpu.SemaphoreType.DMA
    return pl.pallas_call(
        functools.partial(fused_kernel, seq_count, head_count),
        in_specs=[vmem] * 7 + [hbm] * 3,
        out_specs=[vmem] * 4,
        out_shape=[
            jax.ShapeDtypeStruct((rows, columns), jnp.bfloat16),
            jax.ShapeDtypeStruct((8, rows), jnp.float32),
            jax.ShapeDtypeStruct((kept, columns), jnp.bfloat16),
            jax.ShapeDtypeStruct((kept, 2 * HD), jnp.bfloat16),
        ],
        scratch_shapes=[
            pltpu.VMEM((seq_count, rows, 2 * HD), jnp.bfloat16),
            pltpu.VMEM((head_count, kept, depth), jnp.bfloat16),
            pltpu.VMEM((seq_count, rows, rows), jnp.float32),
            pltpu.VMEM((seq_count, 8, rows), jnp.float32),
            pltpu.VMEM((seq_count, 8, rows), jnp.float32),
            pltpu.VMEM((8, rows), jnp.float32),
            pltpu.VMEM((head_count, 8, rows), jnp.float32),
            pltpu.VMEM((head_count, depth, columns), jnp.bfloat16),
            pltpu.VMEM((head_count, depth, HD), jnp.bfloat16),
            pltpu.VMEM((head_count, depth, HD), jnp.bfloat16),
            pltpu.VMEM((kept, columns), jnp.float32),
            pltpu.VMEM((kept, HD), jnp.float32),
            pltpu.VMEM((kept, HD), jnp.float32),
            dma((seq_count,)), dma((seq_count,)), dma((head_count,)), dma((head_count,)),
            dma((seq_count,)), dma((seq_count,)), dma((head_count,)), dma((head_count,)),
            dma((head_count, 3)),
        ],
        compiler_params=pltpu.CompilerParams(
            collective_id=0, has_side_effects=True, vmem_limit_bytes=58 * 1024 * 1024
        ),
    )(q2, kv2, text, x, bias, cosine, sine, w_query, w_key, w_value)


def body(
    q2, k2, v2, hidden, w_query, b_query, w_key, b_key, w_value, b_value, kept_index, block_count, text_rows
):
    rows = q2.shape[0]
    seq_count = lax.axis_size("seq")
    head_count = lax.axis_size("head")
    seq_rank = lax.axis_index("seq")
    first_row = seq_rank * rows
    text = text_rows.shape[0]
    per_device = (rows * seq_count + text) // (2 * seq_count)
    odd = seq_rank % 2

    blocks = rows // BLOCK
    ends = [block_count[0]]
    for b in range(1, blocks):
        ends.append(ends[-1] + block_count[b])
    kept_count = ends[-1]
    base = jnp.where(odd == 1, 2 * per_device - kept_count, 0)
    entry = jnp.arange(rows, dtype=jnp.int32)
    place = base + entry % BLOCK
    live = jnp.zeros((rows,), jnp.bool_)
    for b in range(blocks):
        inside = entry // BLOCK == b
        begin = ends[b] - block_count[b]
        place = place + jnp.where(inside, begin, 0)
        live = live | (inside & (entry % BLOCK < block_count[b]))
    source = (entry // BLOCK) * BLOCK + kept_index

    def window(start, count):
        order = start + jnp.arange(count, dtype=jnp.int32)
        hit = (order[:, None] == place[None, :]) & live[None, :]
        chosen = jnp.sum(jnp.where(hit, source[None, :] + 1, 0), axis=1) - 1
        select = (chosen[:, None] == jnp.arange(rows, dtype=jnp.int32)[None, :]).astype(jnp.bfloat16)
        picked = jnp.dot(select, hidden, preferred_element_type=jnp.float32).astype(jnp.bfloat16)
        return picked, jnp.where(chosen >= 0, chosen + first_row, 0)

    span = min(rows - per_device, per_device)
    swap = [(i, i + 1 - 2 * (i % 2)) for i in range(seq_count)]
    sent_rows, sent_pos = window(jnp.where(odd == 1, per_device - span, per_device), span)
    got_rows = lax.ppermute(sent_rows, "seq", swap)
    got_pos = lax.ppermute(sent_pos, "seq", swap)
    own_rows, own_pos = window(odd * per_device, per_device)
    rest = per_device - span
    low = jnp.where(odd == 1, 0, rest)

    def landed(got):
        shape = ((0, rest),) + ((0, 0),) * (got.ndim - 1)
        back = ((rest, 0),) + ((0, 0),) * (got.ndim - 1)
        return jnp.where(odd == 1, jnp.pad(got, shape), jnp.pad(got, back))

    kept_rows = own_rows + landed(got_rows)
    kept_pos = own_pos + landed(got_pos)
    query_pos = first_row + jnp.arange(rows, dtype=jnp.int32)
    is_text = jnp.any(query_pos[:, None] == text_rows[None, :], axis=1, keepdims=True).astype(jnp.float32)
    half = HD // 2
    freqs = THETA ** (-(jnp.arange(half, dtype=jnp.float32) * 2.0) / HD)
    angles = kept_pos.astype(jnp.float32)[:, None] * freqs[None, :]
    cosine, sine = jnp.cos(angles), jnp.sin(angles)
    cosine = jnp.concatenate([cosine, cosine], axis=1)
    sine = jnp.concatenate([-sine, sine], axis=1)
    bias = jnp.concatenate([b_query, b_key, b_value])[None, :]
    attn2, shares, queries3, pair3 = fused(
        seq_count, head_count, q2, jnp.concatenate([k2, v2], axis=1), is_text, kept_rows, bias, cosine, sine,
        w_query, w_key, w_value,
    )
    importance = jnp.sum(shares, axis=0) * (rows * seq_count / (GROUP * head_count * text))
    pairs3 = lax.all_gather(pair3, "seq", axis=0, tiled=True)
    (attn3,) = attention(seq_rank * per_device, queries3, pairs3[:, :HD], pairs3[:, HD:])
    return (attn2, importance, attn3)


def solution(mesh):
    placed = (
        P("seq", "head"),
        P("seq", "head"),
        P("seq", "head"),
        P("seq", "head"),
        P(None, "head"),
        P("head"),
        P(None, "head"),
        P("head"),
        P(None, "head"),
        P("head"),
        P("seq"),
        P("seq"),
        P(),
    )
    return jax.shard_map(
        body,
        mesh=mesh,
        in_specs=placed,
        out_specs=(P("seq", "head"), P("seq"), P("seq", "head")),
        check_vma=False,
    )
```
